256 devices in a mesh: seq: 256 (over y, z, x, core).
Axes of the slice: x: 4, y: 4, z: 8, core: 2. Of those that a mesh axis runs over, the one named last changes fastest.
Arguments:
- tokens: bfloat16 [131072, 192], P('seq'), may hold values from -6 to 6
- out_grad: bfloat16 [131072, 192], P('seq'), may hold values from -6 to 6
- spread_weight: bfloat16 [384, 768], replicated, may hold values from -0.3125 to 0.3125
- merge_weight: bfloat16 [768, 384], replicated, may hold values from -0.21875 to 0.21875
- switch_bias: float32 [384], replicated, may hold values from -4 to 4
- gate_logit: float32 [384], replicated, may hold values from -1 to 3
Outputs:
- network_out: bfloat16 [131072, 192], P('seq')
- token_grad: bfloat16 [131072, 192], P('seq')
- spread_grad: float32 [384, 768], replicated
- merge_grad: float32 [768, 384], replicated
- bias_grad: float32 [384], replicated
- gate_grad: float32 [384], replicated
The draws below stay inside these ranges and needn't reach their ends.
All inputs are finite; a program needn't handle non-finite values.
Results may differ from the reference program's by a relative error of at most 0.008.
Values may be sent and summed in bfloat16 or wider, within the bound.
No kernel may reach another device: no remote copies, remote signals or barrier semaphores. Data moves between devices by JAX's collectives and lax.ppermute only.
A program may use at most 64 MiB of HBM per device.

```python
import math
import jax
import jax.numpy as jnp
from jax import lax

D = 192
SWITCH = 384
HIDDEN_SIZE = 768
ROWS_DEV = 512
SECTIONS = 4
TOKENS = 131072
N_SEQ = 256


def level_of(key, dims, shards, smallest, largest):
    def one(axis_at, blocks):
        draws = jax.random.uniform(jax.random.fold_in(jax.random.fold_in(key, 6), axis_at), (blocks,), jnp.float32, smallest / len(shards), largest / len(shards))
        return jnp.repeat(jnp.exp(draws), dims[axis_at] // blocks).reshape((-1,) + (1,) * (len(dims) - axis_at - 1))

    factor_of = one(*shards[0])
    for cut in shards[1:]:
        factor_of = factor_of * one(*cut)
    return factor_of


def noise(stream_key, extent, scale, reach, shards=(), held_as=jnp.bfloat16):
    factor_of = level_of(stream_key, extent, shards, -0.22, 0.18) if shards else 1.0
    result = jax.random.normal(stream_key, extent, jnp.float32) * scale * factor_of
    return jnp.minimum(jnp.maximum(result, -reach), reach).astype(held_as)


def setup_inputs(seed: int = 0) -> dict:
    arg_keys = jax.random.split(jax.random.key(seed), 7)
    return {
        "tokens": noise(arg_keys[0], (TOKENS, D), 1.0, 6.0, ((0, 256),)),
        "out_grad": noise(arg_keys[1], (TOKENS, D), 1.0, 6.0, ((0, 256),)),
        "spread_weight": noise(arg_keys[2], (SWITCH, HIDDEN_SIZE), SWITCH ** -0.5, 0.3125),
        "merge_weight": noise(arg_keys[3], (HIDDEN_SIZE, SWITCH), HIDDEN_SIZE ** -0.5, 0.21875),
        "switch_bias": noise(arg_keys[4], (SWITCH,), 1.0, 4.0, (), jnp.float32),
        "gate_logit": jnp.clip(jax.random.uniform(arg_keys[5], (SWITCH,), jnp.float32, -1.0, 3.0), -1.0, 3.0),
    }


sqrt_half = 0.7071067811865476
inv_sqrt_two_pi = 0.3989422804014327

def gelu_exact(values):
    return 0.5 * values * (1.0 + lax.erf(values * sqrt_half))

def gelu_slope(values):
    return 0.5 * (1.0 + lax.erf(values * sqrt_half)) + values * jnp.exp(-0.5 * values * values) * inv_sqrt_two_pi

def normalize(pre_norm):
    centered = pre_norm - lax.optimization_barrier(jnp.mean(pre_norm, -1, keepdims=True))
    inv_scale = lax.rsqrt(lax.optimization_barrier(jnp.mean(centered * centered, -1, keepdims=True)) + 1e-05)
    return (centered * inv_scale, inv_scale)

def switch_forward(paired, spread_weight, merge_weight, switch_bias, gate_logit):
    pre_norm = jnp.dot(paired, spread_weight, preferred_element_type=jnp.float32)
    normed, inv_scale = normalize(pre_norm)
    hidden = gelu_exact(normed).astype(jnp.bfloat16)
    branch = jnp.dot(hidden, merge_weight, preferred_element_type=jnp.float32) + switch_bias
    return (jax.nn.sigmoid(gate_logit) * paired.astype(jnp.float32) + 0.25 * branch).astype(jnp.bfloat16)

def switch_backward(paired, grad_pairs, spread_weight, merge_weight, gate_logit):
    pre_norm = jnp.dot(paired, spread_weight, preferred_element_type=jnp.float32)
    normed, inv_scale = normalize(pre_norm)
    hidden = gelu_exact(normed).astype(jnp.bfloat16)
    grad_rows = grad_pairs.astype(jnp.float32)
    gate_term = lax.optimization_barrier(jnp.sum(grad_rows * paired.astype(jnp.float32), 0))
    bias_term = 0.25 * lax.optimization_barrier(jnp.sum(grad_rows, 0))
    branch_grad = (0.25 * grad_rows).astype(jnp.bfloat16)
    merge_term = lax.dot_general(hidden, branch_grad, (((0,), (0,)), ((), ())), preferred_element_type=jnp.float32)
    hidden_grad = lax.dot_general(branch_grad, merge_weight, (((1,), (1,)), ((), ())), preferred_element_type=jnp.float32)
    normed_grad = hidden_grad * gelu_slope(normed)
    pre_grad = inv_scale * (normed_grad - lax.optimization_barrier(jnp.mean(normed_grad, -1, keepdims=True)) - normed * lax.optimization_barrier(jnp.mean(normed_grad * normed, -1, keepdims=True)))
    pre_grad = pre_grad.astype(jnp.bfloat16)
    spread_term = lax.dot_general(paired, pre_grad, (((0,), (0,)), ((), ())), preferred_element_type=jnp.float32)
    back_rows = lax.dot_general(pre_grad, spread_weight, (((1,), (1,)), ((), ())), preferred_element_type=jnp.float32)
    paired_grad = (jax.nn.sigmoid(gate_logit) * grad_rows + back_rows).astype(jnp.bfloat16)
    return (paired_grad, (spread_term, merge_term, bias_term, gate_term))

def to_pairs(rows, distance):
    viewed = rows.reshape(rows.shape[0] // (2 * distance), 2, distance, rows.shape[1])
    return jnp.concatenate([viewed[:, 0], viewed[:, 1]], -1).reshape(-1, 2 * rows.shape[1])

def from_pairs(paired, distance):
    unit_count = paired.shape[1] // 2
    viewed = paired.reshape(-1, distance, 2 * unit_count)
    return jnp.stack([viewed[..., :unit_count], viewed[..., unit_count:]], 1).reshape(-1, unit_count)

def reference(tokens, out_grad, spread_weight, merge_weight, switch_bias, gate_logit):
    device_bits = N_SEQ.bit_length() - 1
    pair_count = TOKENS // 2
    block_rows = math.gcd(pair_count, 8192)
    block_count = pair_count // block_rows
    current = tokens
    saved = []
    for section_num in range(SECTIONS):
        distance = ROWS_DEV * 2 ** (device_bits - 1 - section_num)
        paired = to_pairs(current, distance)
        saved.append(paired)
        blocks = paired.reshape(block_count, block_rows, -1)
        switched = lax.map(lambda block: switch_forward(block, spread_weight, merge_weight, switch_bias, gate_logit), blocks)
        current = from_pairs(switched.reshape(pair_count, -1), distance)
    network_out = current
    grad_rows = out_grad
    spread_total = jnp.zeros(spread_weight.shape, jnp.float32)
    merge_total = jnp.zeros(merge_weight.shape, jnp.float32)
    bias_total = jnp.zeros(switch_bias.shape, jnp.float32)
    gate_total = jnp.zeros(gate_logit.shape, jnp.float32)
    for section_num in reversed(range(SECTIONS)):
        distance = ROWS_DEV * 2 ** (device_bits - 1 - section_num)
        grad_pairs = to_pairs(grad_rows, distance)
        pair_blocks = saved[section_num].reshape(block_count, block_rows, -1)
        grad_blocks = grad_pairs.reshape(block_count, block_rows, -1)
        paired_grad, term_list = lax.map(lambda both: switch_backward(both[0], both[1], spread_weight, merge_weight, gate_logit), (pair_blocks, grad_blocks))
        spread_total = spread_total + lax.optimization_barrier(jnp.sum(term_list[0], 0))
        merge_total = merge_total + lax.optimization_barrier(jnp.sum(term_list[1], 0))
        bias_total = bias_total + lax.optimization_barrier(jnp.sum(term_list[2], 0))
        gate_total = gate_total + lax.optimization_barrier(jnp.sum(term_list[3], 0))
        grad_rows = from_pairs(paired_grad.reshape(pair_count, -1), distance)
    grad_scale = 1.0 / math.sqrt(TOKENS)
    gate_open = jax.nn.sigmoid(gate_logit)
    return (network_out, grad_rows, spread_total * grad_scale, merge_total * grad_scale, bias_total * grad_scale, gate_total * gate_open * (1.0 - gate_open) * grad_scale)
```

```python
import math

import jax
import jax.numpy as jnp
from jax import lax
from jax.experimental import pallas as pl
from jax.experimental.pallas import tpu as pltpu
from jax.sharding import PartitionSpec as P

SECTIONS = 4
MEMBERS = 16
ROWS = 32
UNITS = 192
SWITCH = 384
HIDDEN = 768
PAIRS = 256
CHUNK = 576
AUX = 8
SLOT = 24
BLOCK = 32

sqrt_half = 0.7071067811865476
inv_sqrt_two_pi = 0.3989422804014327
f32 = jnp.float32
bf16 = jnp.bfloat16


def dot(a, b, ca, cb):
    return lax.dot_general(a, b, (((ca,), (cb,)), ((), ())), preferred_element_type=f32)


def sides(section):
    bit = MEMBERS >> (section + 1)
    lower = [g for g in range(MEMBERS) if not g & bit]
    return lower, [g + bit for g in lower]


def load_rows(ref, members):
    return jnp.concatenate([ref[g] for g in members], 0)


def store_rows(ref, members, value):
    for k, g in enumerate(members):
        ref[g] = value[ROWS * k : ROWS * (k + 1)]


def switch_kernel(
    core,
    packed,
    spread,
    merge,
    bias,
    gate,
    packed_out,
    send,
    keep,
    state,
    grad,
    left,
    right,
    pre,
    normed,
    slope,
    hidden,
    scale,
    dbranch,
    dpre,
):
    gate_open = jax.nn.sigmoid(gate[...])
    gate_left = gate_open[:, :UNITS]
    gate_right = gate_open[:, UNITS:]
    bias_left = 0.25 * bias[:, :UNITS]
    bias_right = 0.25 * bias[:, UNITS:]
    state[...] = packed[:, :, :UNITS]
    grad[...] = packed[:, :, UNITS:]
    for section in range(SECTIONS):
        lower, upper = sides(section)
        base = PAIRS * section
        rows = slice(base, base + PAIRS)
        x_left = load_rows(state, lower)
        x_right = load_rows(state, upper)
        left[rows] = x_left
        right[rows] = x_right
        pre[...] = dot(x_left, spread[:UNITS, :], 1, 0) + dot(x_right, spread[UNITS:, :], 1, 0)

        def forward(block, carry, base=base):
            start = pl.multiple_of(block * BLOCK, BLOCK)
            at = pl.ds(start, BLOCK)
            to = pl.ds(base + start, BLOCK)
            value = pre[at, :]
            centered = value - jnp.mean(value, -1, keepdims=True)
            inv = lax.rsqrt(jnp.mean(centered * centered, -1, keepdims=True) + 1e-05)
            norm = centered * inv
            cdf = 0.5 * (1.0 + lax.erf(norm * sqrt_half))
            normed[to, :] = norm
            slope[to, :] = cdf + norm * jnp.exp(-0.5 * norm * norm) * inv_sqrt_two_pi
            hidden[to, :] = (norm * cdf).astype(bf16)
            scale[to, :] = jnp.broadcast_to(inv, (BLOCK, 128))
            return carry

        lax.fori_loop(0, PAIRS // BLOCK, forward, 0)
        act = hidden[rows, :]
        branch_left = dot(act, merge[:, :UNITS], 1, 0)
        branch_right = dot(act, merge[:, UNITS:], 1, 0)
        out_left = gate_left * x_left.astype(f32) + (0.25 * branch_left + bias_left)
        out_right = gate_right * x_right.astype(f32) + (0.25 * branch_right + bias_right)
        store_rows(state, lower, out_left.astype(bf16))
        store_rows(state, upper, out_right.astype(bf16))
    packed_out[:, :, :UNITS] = state[...]

    bias_sum = [jnp.zeros((1, UNITS), f32)] * 2
    gate_sum = [jnp.zeros((1, UNITS), f32)] * 2
    for section in reversed(range(SECTIONS)):
        lower, upper = sides(section)
        base = PAIRS * section
        rows = slice(base, base + PAIRS)
        d_left = load_rows(grad, lower)
        d_right = load_rows(grad, upper)
        wide_left = d_left.astype(f32)
        wide_right = d_right.astype(f32)
        bias_sum[0] += jnp.sum(wide_left, 0, keepdims=True)
        bias_sum[1] += jnp.sum(wide_right, 0, keepdims=True)
        gate_sum[0] += jnp.sum(wide_left * left[rows].astype(f32), 0, keepdims=True)
        gate_sum[1] += jnp.sum(wide_right * right[rows].astype(f32), 0, keepdims=True)
        b_left = (0.25 * wide_left).astype(bf16)
        b_right = (0.25 * wide_right).astype(bf16)
        dbranch[rows, :UNITS] = b_left
        dbranch[rows, UNITS:] = b_right
        pre[...] = dot(b_left, merge[:, :UNITS], 1, 1) + dot(b_right, merge[:, UNITS:], 1, 1)

        def backward(block, carry, base=base):
            start = pl.multiple_of(block * BLOCK, BLOCK)
            at = pl.ds(start, BLOCK)
            to = pl.ds(base + start, BLOCK)
            norm = normed[to, :]
            dn = pre[at, :] * slope[to, :]
            mean = jnp.mean(dn, -1, keepdims=True)
            along = jnp.mean(dn * norm, -1, keepdims=True)
            inv = scale[to, :][:, :1]
            dpre[to, :] = (inv * (dn - mean - norm * along)).astype(bf16)
            return carry

        lax.fori_loop(0, PAIRS // BLOCK, backward, 0)
        back = dpre[rows, :]
        g_left = gate_left * wide_left + dot(back, spread[:UNITS, :], 1, 1)
        g_right = gate_right * wide_right + dot(back, spread[UNITS:, :], 1, 1)
        store_rows(grad, lower, g_left.astype(bf16))
        store_rows(grad, upper, g_right.astype(bf16))
    packed_out[:, :, UNITS:] = grad[...]

    spread_terms = [dot(left[...], dpre[...], 0, 0), dot(right[...], dpre[...], 0, 0)]
    merge_term = dot(hidden[...], dbranch[...], 0, 0)
    bias_row = 0.25 * jnp.concatenate(bias_sum, 1)
    gate_row = jnp.concatenate(gate_sum, 1)
    aux = jnp.concatenate(
        [row[:, 128 * k : 128 * (k + 1)] for row in (bias_row, gate_row) for k in range(3)]
        + [jnp.zeros((2, 128), f32)],
        0,
    )

    def put_spread(ref):
        for i in range(12):
            col = 128 * (i // 2)
            ref[i // 3, UNITS * (i % 3) : UNITS * (i % 3 + 1), :] = spread_terms[i % 2][
                :, col : col + 128
            ].astype(ref.dtype)
        ref[0, CHUNK:, :] = aux.astype(ref.dtype)
        ref[1:, CHUNK:, :] = jnp.zeros((3, AUX, 128), ref.dtype)

    def put_merge(ref):
        for i in range(12):
            row = UNITS * (i % 4)
            col = 128 * (i // 4)
            ref[i // 3, UNITS * (i % 3) : UNITS * (i % 3 + 1), :] = merge_term[
                row : row + UNITS, col : col + 128
            ].astype(ref.dtype)
        ref[:, CHUNK:, :] = jnp.zeros((4, AUX, 128), ref.dtype)

    @pl.when(core[0] == 0)
    def _():
        put_spread(keep)
        put_merge(send)

    @pl.when(core[0] != 0)
    def _():
        put_merge(keep)
        put_spread(send)


def core_sum_kernel(place, keep, came, own, first, second, third):
    for mask, ref in enumerate((own, first, second, third)):
        chunk = place[0] ^ mask
        ref[...] = (keep[chunk] + came[chunk].astype(f32)).astype(ref.dtype)


def ring_sum_kernel(own, first, second, third, slots):
    total = own[...] + first[...].astype(f32) + (second[...].astype(f32) + third[...].astype(f32))
    slots[: CHUNK + AUX, :] = total.astype(bf16)


def slot_sum_kernel(slots, sums):
    total = slots[0].astype(f32)
    for k in range(1, slots.shape[0]):
        total = total + slots[k].astype(f32)
    sums[...] = jnp.broadcast_to(total.astype(bf16)[None], sums.shape)


def collect_kernel(place, own, first, second, third, half):
    for mask, ref in enumerate((own, first, second, third)):
        half[place[0] ^ mask] = ref[...]


def finish_kernel(core, gate, mine, other, spread, merge, bias, gate_out, *, grad_scale):
    def write(first, second):
        for i in range(12):
            rows = slice(UNITS * (i % 3), UNITS * (i % 3 + 1))
            col = 128 * (i // 2)
            row = UNITS * (i % 2)
            spread[row : row + UNITS, col : col + 128] = (
                first[i // 3, rows, :].astype(f32) * grad_scale
            )
            col = 128 * (i // 4)
            row = UNITS * (i % 4)
            merge[row : row + UNITS, col : col + 128] = (
                second[i // 3, rows, :].astype(f32) * grad_scale
            )
        aux = first[0, CHUNK:, :].astype(f32) * grad_scale
        gate_open = jax.nn.sigmoid(gate[...])
        slope = gate_open * (1.0 - gate_open)
        for k in range(3):
            at = slice(128 * k, 128 * (k + 1))
            bias[:, at] = aux[k : k + 1, :]
            gate_out[:, at] = aux[3 + k : 4 + k, :] * slope[:, at]

    @pl.when(core[0] == 0)
    def _():
        write(mine, other)

    @pl.when(core[0] != 0)
    def _():
        write(other, mine)


def shaped(shape, dtype):
    return jax.ShapeDtypeStruct(shape, dtype)


VMEM = pl.BlockSpec(memory_space=pltpu.VMEM)
SMEM = pl.BlockSpec(memory_space=pltpu.SMEM)


def call(kernel, outs, ins, scalars=0, scratch=(), name=None):
    return pl.pallas_call(
        kernel,
        out_shape=outs,
        in_specs=[SMEM] * scalars + [VMEM] * (len(ins) - scalars),
        out_specs=jax.tree.map(lambda _: VMEM, outs),
        scratch_shapes=list(scratch),
        name=name,
        compiler_params=pltpu.CompilerParams(vmem_limit_bytes=56 * 2**20),
    )(*ins)


def bit_groups(count, bits):
    mask = sum(1 << b for b in bits)
    groups = []
    for base in range(count):
        if base & mask:
            continue
        group = [base]
        for b in sorted(bits):
            group = group + [g | (1 << b) for g in group]
        groups.append(group)
    return groups


def exchange(value, mask):
    return lax.ppermute(value, "seq", [(i, i ^ mask) for i in range(lax.axis_size("seq"))])


def on_device(tokens, out_grad, spread_weight, merge_weight, switch_bias, gate_logit):
    count = lax.axis_size("seq")
    grad_scale = 1.0 / math.sqrt(count * tokens.shape[0])
    position = lax.axis_index("seq")
    core = (position % 2).astype(jnp.int32).reshape(1)
    place = (position // 2 % 4).astype(jnp.int32).reshape(1)
    members = bit_groups(count, (4, 5, 6, 7))
    planes = bit_groups(count, (3, 4, 5, 6, 7))

    def swap_rows(packed):
        return lax.all_to_all(packed, "seq", 0, 0, axis_index_groups=members)

    def swap_slots(slots):
        return lax.all_to_all(slots, "seq", 0, 0, axis_index_groups=planes)

    packed = jnp.concatenate([tokens, out_grad], 1).reshape(MEMBERS, ROWS, SWITCH)
    packed = swap_rows(packed)
    bias = switch_bias.reshape(1, SWITCH)
    gate = gate_logit.reshape(1, SWITCH)
    total = SECTIONS * PAIRS
    half = (4, CHUNK + AUX, 128)
    packed_out, send, keep = call(
        switch_kernel,
        (shaped((MEMBERS, ROWS, SWITCH), bf16), shaped(half, bf16), shaped(half, f32)),
        (core, packed, spread_weight, merge_weight, bias, gate),
        1,
        [
            pltpu.VMEM((MEMBERS, ROWS, UNITS), bf16),
            pltpu.VMEM((MEMBERS, ROWS, UNITS), bf16),
            pltpu.VMEM((total, UNITS), bf16),
            pltpu.VMEM((total, UNITS), bf16),
            pltpu.VMEM((PAIRS, HIDDEN), f32),
            pltpu.VMEM((total, HIDDEN), f32),
            pltpu.VMEM((total, HIDDEN), f32),
            pltpu.VMEM((total, HIDDEN), bf16),
            pltpu.VMEM((total, 128), f32),
            pltpu.VMEM((total, SWITCH), bf16),
            pltpu.VMEM((total, HIDDEN), bf16),
        ],
        name="switch",
    )
    came = exchange(send, 1)
    piece = (CHUNK + AUX, 128)
    own, *others = call(
        core_sum_kernel,
        (shaped(piece, f32),) + (shaped(piece, bf16),) * 3,
        (place, keep, came),
        1,
        name="core_sum",
    )
    others = [exchange(value, 2 * (k + 1)) for k, value in enumerate(others)]
    packed_out = swap_rows(packed_out)
    slots = call(
        ring_sum_kernel, shaped((32 * SLOT, 128), bf16), (own, *others), name="ring_sum"
    )
    slots = swap_slots(slots.reshape(32, SLOT, 128))
    sums = call(slot_sum_kernel, shaped(slots.shape, bf16), (slots,), name="slot_sum")
    sums = swap_slots(sums).reshape(32 * SLOT, 128)[: CHUNK + AUX]
    others = [exchange(sums, 2 * (k + 1)) for k in range(3)]
    mine = call(collect_kernel, shaped(half, bf16), (place, sums, *others), 1, name="collect")
    other = exchange(mine, 1)
    spread_grad, merge_grad, bias_grad, gate_grad = call(
        lambda *refs: finish_kernel(*refs, grad_scale=grad_scale),
        (
            shaped((SWITCH, HIDDEN), f32),
            shaped((HIDDEN, SWITCH), f32),
            shaped((1, SWITCH), f32),
            shaped((1, SWITCH), f32),
        ),
        (core, gate, mine, other),
        1,
        name="finish",
    )
    packed_out = packed_out.reshape(tokens.shape[0], SWITCH)
    return (
        packed_out[:, :UNITS],
        packed_out[:, UNITS:],
        spread_grad,
        merge_grad,
        bias_grad.reshape(SWITCH),
        gate_grad.reshape(SWITCH),
    )


def solution(mesh):
    placed = (P("seq", None), P("seq", None), P(), P(), P(), P())
    return jax.shard_map(
        on_device,
        mesh=mesh,
        in_specs=placed,
        out_specs=(P("seq", None), P("seq", None), P(), P(), P(), P()),
        check_vma=False,
    )
```

```python
import math

import jax
import jax.numpy as jnp
from jax import lax
from jax.experimental import pallas as pl
from jax.experimental.pallas import tpu as pltpu
from jax.sharding import PartitionSpec as P


SECTIONS = 4
MEMBERS = 16
ROWS = 32
UNITS = 192
SWITCH = 384
HIDDEN = 768
PAIRS = 256
CHUNK = 576
AUX = 8
SLOT = 24
BLOCK = 32
ORDER = [4 * i % MEMBERS + i // 4 for i in range(MEMBERS)]

sqrt_half = 0.7071067811865476
inv_sqrt_two_pi = 0.3989422804014327
f32 = jnp.float32
bf16 = jnp.bfloat16


def dot(a, b, ca, cb):
    return lax.dot_general(a, b, (((ca,), (cb,)), ((), ())), preferred_element_type=f32)


def sides(section):
    bit = MEMBERS >> (section + 1)
    lower = [g for g in range(MEMBERS) if not g & bit]
    return lower, [g + bit for g in lower]


def load_rows(ref, members):
    return jnp.concatenate([ref[g] for g in members], 0)


def store_rows(ref, members, value):
    for k, g in enumerate(members):
        ref[g] = value[ROWS * k : ROWS * (k + 1)]


def add_to(ref, section, term):
    if section == SECTIONS - 1:
        ref[...] = term
    else:
        ref[...] += term


def switch_kernel(
    core,
    packed,
    spread,
    merge,
    bias,
    gate,
    packed_out,
    send,
    keep,
    state,
    grad,
    left,
    right,
    pre,
    normed,
    slope,
    hidden,
    scale,
    dbranch,
    dpre,
    spread_sum,
    merge_sum,
):
    gate_open = jax.nn.sigmoid(gate[...])
    gate_left = gate_open[:, :UNITS]
    gate_right = gate_open[:, UNITS:]
    bias_left = 0.25 * bias[:, :UNITS]
    bias_right = 0.25 * bias[:, UNITS:]
    for i, g in enumerate(ORDER):
        state[g] = packed[i, :, :UNITS]
        grad[g] = packed[i, :, UNITS:]
    for section in range(SECTIONS):
        lower, upper = sides(section)
        base = PAIRS * section
        rows = slice(base, base + PAIRS)
        x_left = load_rows(state, lower)
        x_right = load_rows(state, upper)
        left[rows] = x_left
        right[rows] = x_right
        pre[...] = dot(x_left, spread[:UNITS, :], 1, 0) + dot(x_right, spread[UNITS:, :], 1, 0)

        def forward(block, carry, base=base):
            start = pl.multiple_of(block * BLOCK, BLOCK)
            at = pl.ds(start, BLOCK)
            to = pl.ds(base + start, BLOCK)
            value = pre[at, :]
            centered = value - jnp.mean(value, -1, keepdims=True)
            inv = lax.rsqrt(jnp.mean(centered * centered, -1, keepdims=True) + 1e-05)
            norm = centered * inv
            cdf = 0.5 * (1.0 + lax.erf(norm * sqrt_half))
            normed[to, :] = norm
            slope[to, :] = cdf + norm * jnp.exp(-0.5 * norm * norm) * inv_sqrt_two_pi
            hidden[to, :] = (norm * cdf).astype(bf16)
            scale[to, :] = jnp.broadcast_to(inv, (BLOCK, 128))
            return carry

        lax.fori_loop(0, PAIRS // BLOCK, forward, 0, unroll=PAIRS // BLOCK)
        act = hidden[rows, :]
        branch_left = dot(act, merge[:, :UNITS], 1, 0)
        branch_right = dot(act, merge[:, UNITS:], 1, 0)
        out_left = gate_left * x_left.astype(f32) + (0.25 * branch_left + bias_left)
        out_right = gate_right * x_right.astype(f32) + (0.25 * branch_right + bias_right)
        store_rows(state, lower, out_left.astype(bf16))
        store_rows(state, upper, out_right.astype(bf16))
    for i, g in enumerate(ORDER):
        packed_out[i, :, :UNITS] = state[g]

    bias_sum = [jnp.zeros((1, UNITS), f32)] * 2
    gate_sum = [jnp.zeros((1, UNITS), f32)] * 2
    for section in reversed(range(SECTIONS)):
        lower, upper = sides(section)
        base = PAIRS * section
        rows = slice(base, base + PAIRS)
        d_left = load_rows(grad, lower)
        d_right = load_rows(grad, upper)
        wide_left = d_left.astype(f32)
        wide_right = d_right.astype(f32)
        bias_sum[0] += jnp.sum(wide_left, 0, keepdims=True)
        bias_sum[1] += jnp.sum(wide_right, 0, keepdims=True)
        gate_sum[0] += jnp.sum(wide_left * left[rows].astype(f32), 0, keepdims=True)
        gate_sum[1] += jnp.sum(wide_right * right[rows].astype(f32), 0, keepdims=True)
        b_left = (0.25 * wide_left).astype(bf16)
        b_right = (0.25 * wide_right).astype(bf16)
        dbranch[rows, :UNITS] = b_left
        dbranch[rows, UNITS:] = b_right
        pre[...] = dot(b_left, merge[:, :UNITS], 1, 1) + dot(b_right, merge[:, UNITS:], 1, 1)
        add_to(merge_sum, section, dot(hidden[rows, :], dbranch[rows, :], 0, 0))

        def backward(block, carry, base=base):
            start = pl.multiple_of(block * BLOCK, BLOCK)
            at = pl.ds(start, BLOCK)
            to = pl.ds(base + start, BLOCK)
            norm = normed[to, :]
            dn = pre[at, :] * slope[to, :]
            mean = jnp.mean(dn, -1, keepdims=True)
            along = jnp.mean(dn * norm, -1, keepdims=True)
            inv = scale[to, :][:, :1]
            dpre[to, :] = (inv * (dn - mean - norm * along)).astype(bf16)
            return carry

        lax.fori_loop(0, PAIRS // BLOCK, backward, 0, unroll=PAIRS // BLOCK)
        back = dpre[rows, :]
        g_left = gate_left * wide_left + dot(back, spread[:UNITS, :], 1, 1)
        g_right = gate_right * wide_right + dot(back, spread[UNITS:, :], 1, 1)
        store_rows(grad, lower, g_left.astype(bf16))
        store_rows(grad, upper, g_right.astype(bf16))
        add_to(spread_sum.at[:UNITS], section, dot(left[rows], back, 0, 0))
        add_to(spread_sum.at[UNITS:], section, dot(right[rows], back, 0, 0))
    for i, g in enumerate(ORDER):
        packed_out[i, :, UNITS:] = grad[g]

    bias_row = 0.25 * jnp.concatenate(bias_sum, 1)
    gate_row = jnp.concatenate(gate_sum, 1)
    aux = jnp.concatenate(
        [row[:, 128 * k : 128 * (k + 1)] for row in (bias_row, gate_row) for k in range(3)]
        + [jnp.zeros((2, 128), f32)],
        0,
    )

    def put_spread(ref):
        for q in range(4):
            for c in range(6):
                ref[q, 96 * c : 96 * (c + 1), :] = spread_sum[
                    96 * q : 96 * (q + 1), 128 * c : 128 * (c + 1)
                ].astype(ref.dtype)
        ref[0, CHUNK:, :] = aux.astype(ref.dtype)
        ref[1:, CHUNK:, :] = jnp.zeros((3, AUX, 128), ref.dtype)

    def put_merge(ref):
        for q in range(4):
            for c in range(3):
                ref[q, 192 * c : 192 * (c + 1), :] = merge_sum[
                    192 * q : 192 * (q + 1), 128 * c : 128 * (c + 1)
                ].astype(ref.dtype)
        ref[:, CHUNK:, :] = jnp.zeros((4, AUX, 128), ref.dtype)

    @pl.when(core[0] == 0)
    def _():
        put_spread(keep)
        put_merge(send)

    @pl.when(core[0] != 0)
    def _():
        put_merge(keep)
        put_spread(send)


def pack_kernel(tokens, out_grad, packed):
    rows = jnp.concatenate([tokens[...], out_grad[...]], 0).T
    for i, g in enumerate(ORDER):
        packed[i] = rows[ROWS * g : ROWS * (g + 1)]


def unpack_kernel(packed, network_out, token_grad):
    places = [ORDER.index(g) for g in range(MEMBERS)]
    columns = jnp.concatenate([packed[i] for i in places], 0).T
    network_out[...] = columns[:UNITS]
    token_grad[...] = columns[UNITS:]


def core_sum_kernel(place, keep, came, own, first, second, third):
    for mask, ref in enumerate((own, first, second, third)):
        chunk = place[0] ^ mask
        ref[...] = (keep[chunk] + came[chunk].astype(f32)).astype(ref.dtype)


def ring_sum_kernel(own, first, second, third, slots):
    total = own[...] + first[...].astype(f32) + (second[...].astype(f32) + third[...].astype(f32))
    slots[: CHUNK + AUX, :] = total.astype(bf16)
    slots[CHUNK + AUX :, :] = jnp.zeros((32 * SLOT - CHUNK - AUX, 128), bf16)


def slot_sum_kernel(slots, sums):
    total = slots[0].astype(f32)
    for k in range(1, slots.shape[0]):
        total = total + slots[k].astype(f32)
    sums[...] = jnp.broadcast_to(total.astype(bf16)[None], sums.shape)


def finish_kernel(core, place, gate, *refs, grad_scale):
    mine, theirs = refs[:4], refs[4:8]
    spread, merge, bias, gate_out = refs[8:]

    def write(firsts, seconds):
        for mask in range(4):
            chunk = place[0] ^ mask
            rows = pl.ds(pl.multiple_of(96 * chunk, 96), 96)
            for c in range(6):
                spread[rows, 128 * c : 128 * (c + 1)] = (
                    firsts[mask][96 * c : 96 * (c + 1), :].astype(f32) * grad_scale
                )
            rows = pl.ds(pl.multiple_of(192 * chunk, 192), 192)
            for c in range(3):
                merge[rows, 128 * c : 128 * (c + 1)] = (
                    seconds[mask][192 * c : 192 * (c + 1), :].astype(f32) * grad_scale
                )

            @pl.when(chunk == 0)
            def _(mask=mask):
                aux = firsts[mask][CHUNK:, :].astype(f32) * grad_scale
                gate_open = jax.nn.sigmoid(gate[...])
                slope = gate_open * (1.0 - gate_open)
                for k in range(3):
                    at = slice(128 * k, 128 * (k + 1))
                    bias[at] = aux[k, :]
                    gate_out[at] = aux[3 + k, :] * slope[0, at]

    @pl.when(core[0] == 0)
    def _():
        write(mine, theirs)

    @pl.when(core[0] != 0)
    def _():
        write(theirs, mine)


def shaped(shape, dtype):
    return jax.ShapeDtypeStruct(shape, dtype)


def near(shape, dtype):
    return pltpu.VMEM(shape, dtype)


VMEM = pl.BlockSpec(memory_space=pltpu.VMEM)
SMEM = pl.BlockSpec(memory_space=pltpu.SMEM)


def call(kernel, outs, ins, scalars=0, scratch=(), far=False):
    arrays = ins[scalars:]
    space = pltpu.HBM if far else pltpu.VMEM
    arrays = [pltpu.with_memory_space_constraint(a, space) for a in arrays]
    return pl.pallas_call(
        kernel,
        out_shape=outs,
        in_specs=[SMEM] * scalars + [VMEM] * len(arrays),
        out_specs=tuple(VMEM for _ in outs) if isinstance(outs, tuple) else VMEM,
        scratch_shapes=list(scratch),
        compiler_params=pltpu.CompilerParams(vmem_limit_bytes=40 * 2**20),
    )(*ins[:scalars], *arrays)


def bit_groups(count, bits):
    stride = 2 ** (len(bits) - 2)
    mask = sum(1 << b for b in bits)
    groups = []
    for base in range(count):
        if base & mask:
            continue
        group = [base]
        for b in sorted(bits):
            group = group + [g | (1 << b) for g in group]
        groups.append([group[stride * i % len(group) + i // 4] for i in range(len(group))])
    return groups


def exchange(value, mask):
    return lax.ppermute(value, "seq", [(i, i ^ mask) for i in range(lax.axis_size("seq"))])


def step(tokens, out_grad, spread_weight, merge_weight, switch_bias, gate_logit):
    count = lax.axis_size("seq")
    grad_scale = 1.0 / math.sqrt(count * tokens.shape[0])
    position = lax.axis_index("seq")
    core = (position % 2).astype(jnp.int32).reshape(1)
    place = (position // 2 % 4).astype(jnp.int32).reshape(1)
    members = bit_groups(count, (4, 5, 6, 7))
    planes = bit_groups(count, (3, 4, 5, 6, 7))

    def swap_rows(packed):
        return lax.all_to_all(packed, "seq", 0, 0, axis_index_groups=members)

    def swap_slots(slots):
        return lax.all_to_all(slots, "seq", 0, 0, axis_index_groups=planes)

    rows = tokens.shape[0]
    packed = call(
        pack_kernel, near((MEMBERS, ROWS, SWITCH), bf16), (tokens.T, out_grad.T), far=True
    )
    packed = swap_rows(packed)
    bias = switch_bias.reshape(1, SWITCH)
    gate = gate_logit.reshape(1, SWITCH)
    total = SECTIONS * PAIRS
    half = (4, CHUNK + AUX, 128)
    packed_out, send, keep = call(
        switch_kernel,
        (near((MEMBERS, ROWS, SWITCH), bf16), near(half, bf16), near(half, f32)),
        (core, packed, spread_weight, merge_weight, bias, gate),
        1,
        [
            pltpu.VMEM((MEMBERS, ROWS, UNITS), bf16),
            pltpu.VMEM((MEMBERS, ROWS, UNITS), bf16),
            pltpu.VMEM((total, UNITS), bf16),
            pltpu.VMEM((total, UNITS), bf16),
            pltpu.VMEM((PAIRS, HIDDEN), f32),
            pltpu.VMEM((total, HIDDEN), f32),
            pltpu.VMEM((total, HIDDEN), f32),
            pltpu.VMEM((total, HIDDEN), bf16),
            pltpu.VMEM((total, 128), f32),
            pltpu.VMEM((total, SWITCH), bf16),
            pltpu.VMEM((total, HIDDEN), bf16),
            pltpu.VMEM((SWITCH, HIDDEN), f32),
            pltpu.VMEM((HIDDEN, SWITCH), f32),
        ],
    )
    came = exchange(send, 1)
    piece = (CHUNK + AUX, 128)
    own, *others = call(
        core_sum_kernel, (near(piece, f32),) + (near(piece, bf16),) * 3, (place, keep, came), 1
    )
    others = [exchange(value, 2 * (k + 1)) for k, value in enumerate(others)]
    packed_out = swap_rows(packed_out)
    slots = call(ring_sum_kernel, near((32 * SLOT, 128), bf16), (own, *others))
    slots = swap_slots(slots.reshape(32, SLOT, 128))
    sums = call(slot_sum_kernel, near(slots.shape, bf16), (slots,))
    sums = swap_slots(sums)
    sums = sums.reshape(32 * SLOT, 128)[: CHUNK + AUX]
    mine = [sums]
    mine += [exchange(sums, 2 * (k + 1)) for k in range(3)]
    theirs = [exchange(value, 1) for value in mine]
    network_out, token_grad = call(unpack_kernel, (shaped((UNITS, rows), bf16),) * 2, (packed_out,))
    spread_grad, merge_grad, bias_grad, gate_grad = call(
        lambda *refs: finish_kernel(*refs, grad_scale=grad_scale),
        (
            shaped((SWITCH, HIDDEN), f32),
            shaped((HIDDEN, SWITCH), f32),
            shaped((SWITCH,), f32),
            shaped((SWITCH,), f32),
        ),
        (core, place, gate, *mine, *theirs),
        2,
    )
    return (network_out.T, token_grad.T, spread_grad, merge_grad, bias_grad, gate_grad)


def solution(mesh):
    placed = (P("seq", None), P("seq", None), P(), P(), P(), P())
    return jax.shard_map(
        step,
        mesh=mesh,
        in_specs=placed,
        out_specs=(P("seq", None), P("seq", None), P(), P(), P(), P()),
        check_vma=False,
    )
```

```python
import math

import jax
import jax.numpy as jnp
from jax import lax
from jax.experimental import pallas as pl
from jax.experimental.pallas import tpu as pltpu
from jax.sharding import PartitionSpec as P


SECTIONS = 4
MEMBERS = 16
ROWS = 32
UNITS = 192
SWITCH = 384
HIDDEN = 768
PAIRS = 256
PIECE = 144
AUX = 8
BLOCK = 32
ORDER = list(reversed(range(MEMBERS)))

sqrt_half = 0.7071067811865476
inv_sqrt_two_pi = 0.3989422804014327
f32 = jnp.float32
bf16 = jnp.bfloat16


def dot(a, b, ca, cb):
    return lax.dot_general(a, b, (((ca,), (cb,)), ((), ())), preferred_element_type=f32)


def sides(section):
    bit = MEMBERS >> (section + 1)
    lower = [g for g in range(MEMBERS) if not g & bit]
    return lower, [g + bit for g in lower]


def load_rows(ref, members):
    return jnp.concatenate([ref[g] for g in members], 0)


def store_rows(ref, members, value):
    for k, g in enumerate(members):
        ref[g] = value[ROWS * k : ROWS * (k + 1)]


def add_to(ref, section, term):
    if section == SECTIONS - 1:
        ref[...] = term
    else:
        ref[...] += term


def switch_kernel(
    core,
    packed,
    spread,
    merge,
    bias,
    gate,
    packed_out,
    send,
    keep,
    state,
    grad,
    paired,
    pre,
    normed,
    slope,
    hidden,
    scale,
    dbranch,
    dpre,
    spread_sum,
    merge_sum,
):
    gate_open = jax.nn.sigmoid(gate[...].reshape(1, SWITCH))
    bias_all = 0.25 * bias[...].reshape(1, SWITCH)
    for i, g in enumerate(ORDER):
        state[g] = packed[i, :, :UNITS]
        grad[g] = packed[i, :, UNITS:]
    for section in range(SECTIONS):
        lower, upper = sides(section)
        base = PAIRS * section
        rows = slice(base, base + PAIRS)
        paired[rows, :UNITS] = load_rows(state, lower)
        paired[rows, UNITS:] = load_rows(state, upper)
        here = paired[rows, :]
        pre[...] = dot(here, spread[...], 1, 0)
        for start in range(0, PAIRS, BLOCK):
            at = slice(start, start + BLOCK)
            to = slice(base + start, base + start + BLOCK)
            value = pre[at, :]
            centered = value - jnp.mean(value, -1, keepdims=True)
            inv = lax.rsqrt(jnp.mean(centered * centered, -1, keepdims=True) + 1e-05)
            norm = centered * inv
            cdf = 0.5 * (1.0 + lax.erf(norm * sqrt_half))
            normed[to, :] = norm
            slope[to, :] = cdf + norm * jnp.exp(-0.5 * norm * norm) * inv_sqrt_two_pi
            hidden[to, :] = (norm * cdf).astype(bf16)
            scale[to, :] = jnp.broadcast_to(inv, (BLOCK, 128))
        branch = dot(hidden[rows, :], merge[...], 1, 0)
        out = (gate_open * here.astype(f32) + (0.25 * branch + bias_all)).astype(bf16)
        store_rows(state, lower, out[:, :UNITS])
        store_rows(state, upper, out[:, UNITS:])
    for i, g in enumerate(ORDER):
        packed_out[i, :, :UNITS] = state[g]

    bias_sum = jnp.zeros((1, SWITCH), f32)
    gate_sum = jnp.zeros((1, SWITCH), f32)
    for section in reversed(range(SECTIONS)):
        lower, upper = sides(section)
        base = PAIRS * section
        rows = slice(base, base + PAIRS)
        dbranch[rows, :UNITS] = load_rows(grad, lower)
        dbranch[rows, UNITS:] = load_rows(grad, upper)
        wide = dbranch[rows, :].astype(f32)
        bias_sum += jnp.sum(wide, 0, keepdims=True)
        gate_sum += jnp.sum(wide * paired[rows, :].astype(f32), 0, keepdims=True)
        quarter = (0.25 * wide).astype(bf16)
        dbranch[rows, :] = quarter
        pre[...] = dot(quarter, merge[...], 1, 1)
        add_to(merge_sum, section, dot(hidden[rows, :], quarter, 0, 0))
        for start in range(0, PAIRS, BLOCK):
            at = slice(start, start + BLOCK)
            to = slice(base + start, base + start + BLOCK)
            norm = normed[to, :]
            dn = pre[at, :] * slope[to, :]
            mean = jnp.mean(dn, -1, keepdims=True)
            along = jnp.mean(dn * norm, -1, keepdims=True)
            inv = scale[to, :][:, :1]
            dpre[at, :] = (inv * (dn - mean - norm * along)).astype(bf16)
        back = dpre[...]
        total = (gate_open * wide + dot(back, spread[...], 1, 1)).astype(bf16)
        store_rows(grad, lower, total[:, :UNITS])
        store_rows(grad, upper, total[:, UNITS:])
        add_to(spread_sum, section, dot(paired[rows, :], back, 0, 0))
    for i, g in enumerate(ORDER):
        packed_out[i, :, UNITS:] = grad[g]

    bias_row = 0.25 * bias_sum
    gate_row = gate_sum
    aux = jnp.concatenate(
        [row[:, 128 * k : 128 * (k + 1)] for row in (bias_row, gate_row) for k in range(3)]
        + [jnp.zeros((2, 128), f32)],
        0,
    )

    def put_spread(ref):
        for p in range(16):
            for c in range(6):
                ref[p, 24 * c : 24 * (c + 1), :] = spread_sum[
                    24 * p : 24 * (p + 1), 128 * c : 128 * (c + 1)
                ].astype(ref.dtype)
        ref[0, PIECE:, :] = aux.astype(ref.dtype)
        ref[1:, PIECE:, :] = jnp.zeros((15, AUX, 128), ref.dtype)

    def put_merge(ref):
        for p in range(16):
            for c in range(3):
                ref[p, 48 * c : 48 * (c + 1), :] = merge_sum[
                    48 * p : 48 * (p + 1), 128 * c : 128 * (c + 1)
                ].astype(ref.dtype)
        ref[:, PIECE:, :] = jnp.zeros((16, AUX, 128), ref.dtype)

    @pl.when(core[0] == 0)
    def _():
        put_spread(keep)
        put_merge(send)

    @pl.when(core[0] != 0)
    def _():
        put_merge(keep)
        put_spread(send)


def pack_kernel(tokens, out_grad, packed):
    rows = jnp.concatenate([tokens[...], out_grad[...]], 0).T
    for i, g in enumerate(ORDER):
        packed[i] = rows[ROWS * g : ROWS * (g + 1)]


def unpack_kernel(packed, network_out, token_grad):
    places = [ORDER.index(g) for g in range(MEMBERS)]
    columns = jnp.concatenate([packed[i] for i in places], 0).T
    network_out[...] = columns[:UNITS]
    token_grad[...] = columns[UNITS:]


def core_sum_kernel(keep, came, pieces):
    pieces[...] = (keep[...] + came[...].astype(f32)).astype(bf16)


def piece_sum_kernel(pieces, total):
    value = pieces[0].astype(f32)
    for k in range(1, pieces.shape[0]):
        value = value + pieces[k].astype(f32)
    total[...] = value.astype(bf16)


def pair_sum_kernel(own, came, total):
    value = (own[...].astype(f32) + came[...].astype(f32)).astype(bf16)
    total[...] = jnp.broadcast_to(value, total.shape)


def finish_kernel(core, gate, mine, theirs, spread, merge, bias, gate_out, *, grad_scale):
    def write(first, second):
        for p in range(16):
            rows = slice(24 * p, 24 * (p + 1))
            for c in range(6):
                spread[rows, 128 * c : 128 * (c + 1)] = (
                    first[p, 24 * c : 24 * (c + 1), :].astype(f32) * grad_scale
                )
            rows = slice(48 * p, 48 * (p + 1))
            for c in range(3):
                merge[rows, 128 * c : 128 * (c + 1)] = (
                    second[p, 48 * c : 48 * (c + 1), :].astype(f32) * grad_scale
                )
        aux = first[0, PIECE:, :].astype(f32) * grad_scale
        gate_open = jax.nn.sigmoid(gate[...].reshape(1, SWITCH))
        slope = gate_open * (1.0 - gate_open)
        for k in range(3):
            at = slice(128 * k, 128 * (k + 1))
            bias[at] = aux[k, :]
            gate_out[at] = aux[3 + k, :] * slope[0, at]

    @pl.when(core[0] == 0)
    def _():
        write(mine, theirs)

    @pl.when(core[0] != 0)
    def _():
        write(theirs, mine)


def shaped(shape, dtype):
    return jax.ShapeDtypeStruct(shape, dtype)


def near(shape, dtype):
    return pltpu.VMEM(shape, dtype)


VMEM = pl.BlockSpec(memory_space=pltpu.VMEM)
SMEM = pl.BlockSpec(memory_space=pltpu.SMEM)


def call(kernel, outs, ins, scalars=0, scratch=(), far=False):
    arrays = ins[scalars:]
    space = pltpu.HBM if far else pltpu.VMEM
    arrays = [pltpu.with_memory_space_constraint(a, space) for a in arrays]
    return pl.pallas_call(
        kernel,
        out_shape=outs,
        in_specs=[SMEM] * scalars + [VMEM] * len(arrays),
        out_specs=tuple(VMEM for _ in outs) if isinstance(outs, tuple) else VMEM,
        scratch_shapes=list(scratch),
        compiler_params=pltpu.CompilerParams(vmem_limit_bytes=40 * 2**20),
    )(*ins[:scalars], *arrays)


def bit_groups(count, bits):
    mask = sum(1 << b for b in bits)
    groups = []
    for base in range(count):
        if base & mask:
            continue
        group = [base]
        for b in sorted(bits):
            group = group + [g | (1 << b) for g in group]
        groups.append(group)
    return groups


def exchange(value, mask):
    return lax.ppermute(value, "seq", [(i, i ^ mask) for i in range(lax.axis_size("seq"))])


def step(tokens, out_grad, spread_weight, merge_weight, switch_bias, gate_logit):
    count = lax.axis_size("seq")
    grad_scale = 1.0 / math.sqrt(count * tokens.shape[0])
    position = lax.axis_index("seq")
    core = (position % 2).astype(jnp.int32).reshape(1)
    members = [[group[g] for g in ORDER] for group in bit_groups(count, (4, 5, 6, 7))]
    planes = bit_groups(count, (1, 2, 6, 7))

    def swap_rows(packed):
        return lax.all_to_all(packed, "seq", 0, 0, axis_index_groups=members)

    def swap_slots(slots):
        return lax.all_to_all(slots, "seq", 0, 0, axis_index_groups=planes)

    rows = tokens.shape[0]
    packed = call(
        pack_kernel,
        near((MEMBERS, ROWS, SWITCH), bf16),
        (tokens.T, out_grad.T),
        far=True,
    )
    packed = swap_rows(packed)
    total = SECTIONS * PAIRS
    piece = (PIECE + AUX, 128)
    half = (16, *piece)
    packed_out, send, keep = call(
        switch_kernel,
        (near((MEMBERS, ROWS, SWITCH), bf16), near(half, bf16), near(half, f32)),
        (core, packed, spread_weight, merge_weight, switch_bias, gate_logit),
        1,
        [
            pltpu.VMEM((MEMBERS, ROWS, UNITS), bf16),
            pltpu.VMEM((MEMBERS, ROWS, UNITS), bf16),
            pltpu.VMEM((total, SWITCH), bf16),
            pltpu.VMEM((PAIRS, HIDDEN), f32),
            pltpu.VMEM((total, HIDDEN), f32),
            pltpu.VMEM((total, HIDDEN), f32),
            pltpu.VMEM((total, HIDDEN), bf16),
            pltpu.VMEM((total, 128), f32),
            pltpu.VMEM((total, SWITCH), bf16),
            pltpu.VMEM((PAIRS, HIDDEN), bf16),
            pltpu.VMEM((SWITCH, HIDDEN), f32),
            pltpu.VMEM((HIDDEN, SWITCH), f32),
        ],
    )
    came = exchange(send, 1)
    pieces = call(core_sum_kernel, near(half, bf16), (keep, came))
    pieces = swap_slots(pieces)
    summed = call(piece_sum_kernel, near(piece, bf16), (pieces,))
    came = exchange(summed, 8)
    packed_out = swap_rows(packed_out)
    summed = call(pair_sum_kernel, near(piece, bf16), (summed, came))
    came = exchange(summed, 16)
    summed = call(pair_sum_kernel, near(piece, bf16), (summed, came))
    came = exchange(summed, 32)
    pieces = call(pair_sum_kernel, near(half, bf16), (summed, came))
    mine = swap_slots(pieces)
    theirs = exchange(mine, 1)
    network_out, token_grad = call(
        unpack_kernel, (shaped((UNITS, rows), bf16),) * 2, (packed_out,)
    )
    spread_grad, merge_grad, bias_grad, gate_grad = call(
        lambda *refs: finish_kernel(*refs, grad_scale=grad_scale),
        (
            shaped((SWITCH, HIDDEN), f32),
            shaped((HIDDEN, SWITCH), f32),
            shaped((SWITCH,), f32),
            shaped((SWITCH,), f32),
        ),
        (core, gate_logit, mine, theirs),
        1,
    )
    return (network_out.T, token_grad.T, spread_grad, merge_grad, bias_grad, gate_grad)


def solution(mesh):
    placed = (P("seq", None), P("seq", None), P(), P(), P(), P())
    return jax.shard_map(
        step,
        mesh=mesh,
        in_specs=placed,
        out_specs=(P("seq", None), P("seq", None), P(), P(), P(), P()),
        check_vma=False,
    )
```

```python
import math

import jax
import jax.numpy as jnp
from jax import lax
from jax.experimental import pallas as pl
from jax.experimental.pallas import tpu as pltpu
from jax.sharding import PartitionSpec as P


SECTIONS = 4
MEMBERS = 16
ROWS = 32
UNITS = 192
SWITCH = 384
HIDDEN = 768
PAIRS = 256
PIECE = 144
AUX = 8
BLOCK = 32
ORDER = list(reversed(range(MEMBERS)))

sqrt_half = 0.7071067811865476
inv_sqrt_two_pi = 0.3989422804014327
f32 = jnp.float32
bf16 = jnp.bfloat16


def dot(a, b, ca, cb):
    return lax.dot_general(a, b, (((ca,), (cb,)), ((), ())), preferred_element_type=f32)


def sides(section):
    bit = MEMBERS >> (section + 1)
    lower = [g for g in range(MEMBERS) if not g & bit]
    return lower, [g + bit for g in lower]


def load_rows(ref, members):
    return jnp.concatenate([ref[g] for g in members], 0)


def store_rows(ref, members, value):
    for k, g in enumerate(members):
        ref[g] = value[ROWS * k : ROWS * (k + 1)]


def add_to(ref, section, term):
    if section == SECTIONS - 1:
        ref[...] = term
    else:
        ref[...] += term


def switch_kernel(
    core,
    packed,
    spread,
    merge,
    bias,
    gate,
    packed_out,
    send,
    keep,
    state,
    grad,
    paired,
    pre,
    normed,
    slope,
    hidden,
    scale,
    dbranch,
    dpre,
    spread_sum,
    merge_sum,
):
    gate_open = jax.nn.sigmoid(gate[...].reshape(1, SWITCH))
    bias_all = 0.25 * bias[...].reshape(1, SWITCH)
    for i, g in enumerate(ORDER):
        state[g] = packed[i, :, :UNITS]
        grad[g] = packed[i, :, UNITS:]
    for section in range(SECTIONS):
        lower, upper = sides(section)
        base = PAIRS * section
        rows = slice(base, base + PAIRS)
        paired[rows, :UNITS] = load_rows(state, lower)
        paired[rows, UNITS:] = load_rows(state, upper)
        here = paired[rows, :]
        pre[...] = dot(here, spread[...], 1, 0)
        for start in range(0, PAIRS, BLOCK):
            at = slice(start, start + BLOCK)
            to = slice(base + start, base + start + BLOCK)
            value = pre[at, :]
            centered = value - jnp.mean(value, -1, keepdims=True)
            inv = lax.rsqrt(jnp.mean(centered * centered, -1, keepdims=True) + 1e-05)
            norm = centered * inv
            cdf = 0.5 * (1.0 + lax.erf(norm * sqrt_half))
            normed[to, :] = norm
            slope[to, :] = cdf + norm * jnp.exp(-0.5 * norm * norm) * inv_sqrt_two_pi
            hidden[to, :] = (norm * cdf).astype(bf16)
            scale[to, :] = jnp.broadcast_to(inv, (BLOCK, 128))
        branch = dot(hidden[rows, :], merge[...], 1, 0)
        out = (gate_open * here.astype(f32) + (0.25 * branch + bias_all)).astype(bf16)
        store_rows(state, lower, out[:, :UNITS])
        store_rows(state, upper, out[:, UNITS:])
    for i, g in enumerate(ORDER):
        packed_out[i, :, :UNITS] = state[g]

    bias_sum = jnp.zeros((1, SWITCH), f32)
    gate_sum = jnp.zeros((1, SWITCH), f32)
    for section in reversed(range(SECTIONS)):
        lower, upper = sides(section)
        base = PAIRS * section
        rows = slice(base, base + PAIRS)
        dbranch[rows, :UNITS] = load_rows(grad, lower)
        dbranch[rows, UNITS:] = load_rows(grad, upper)
        wide = dbranch[rows, :].astype(f32)
        bias_sum += jnp.sum(wide, 0, keepdims=True)
        gate_sum += jnp.sum(wide * paired[rows, :].astype(f32), 0, keepdims=True)
        quarter = (0.25 * wide).astype(bf16)
        dbranch[rows, :] = quarter
        pre[...] = dot(quarter, merge[...], 1, 1)
        add_to(merge_sum, section, dot(hidden[rows, :], quarter, 0, 0))
        for start in range(0, PAIRS, BLOCK):
            at = slice(start, start + BLOCK)
            to = slice(base + start, base + start + BLOCK)
            norm = normed[to, :]
            dn = pre[at, :] * slope[to, :]
            mean = jnp.mean(dn, -1, keepdims=True)
            along = jnp.mean(dn * norm, -1, keepdims=True)
            inv = scale[to, :][:, :1]
            dpre[at, :] = (inv * (dn - mean - norm * along)).astype(bf16)
        back = dpre[...]
        total = (gate_open * wide + dot(back, spread[...], 1, 1)).astype(bf16)
        store_rows(grad, lower, total[:, :UNITS])
        store_rows(grad, upper, total[:, UNITS:])
        add_to(spread_sum, section, dot(paired[rows, :], back, 0, 0))
    for i, g in enumerate(ORDER):
        packed_out[i, :, UNITS:] = grad[g]

    bias_row = 0.25 * bias_sum
    gate_row = gate_sum
    aux = jnp.concatenate(
        [row[:, 128 * k : 128 * (k + 1)] for row in (bias_row, gate_row) for k in range(3)]
        + [jnp.zeros((2, 128), f32)],
        0,
    )

    def put_spread(ref):
        for p in range(16):
            for c in range(6):
                ref[p, 24 * c : 24 * (c + 1), :] = spread_sum[
                    24 * p : 24 * (p + 1), 128 * c : 128 * (c + 1)
                ].astype(ref.dtype)
        ref[0, PIECE:, :] = aux.astype(ref.dtype)
        ref[1:, PIECE:, :] = jnp.zeros((15, AUX, 128), ref.dtype)

    def put_merge(ref):
        for p in range(16):
            for c in range(3):
                ref[p, 48 * c : 48 * (c + 1), :] = merge_sum[
                    48 * p : 48 * (p + 1), 128 * c : 128 * (c + 1)
                ].astype(ref.dtype)
        ref[:, PIECE:, :] = jnp.zeros((16, AUX, 128), ref.dtype)

    @pl.when(core[0] == 0)
    def _():
        put_spread(keep)
        put_merge(send)

    @pl.when(core[0] != 0)
    def _():
        put_merge(keep)
        put_spread(send)


def pack_kernel(tokens, out_grad, packed):
    rows = jnp.concatenate([tokens[...], out_grad[...]], 0).T
    for i, g in enumerate(ORDER):
        packed[i] = rows[ROWS * g : ROWS * (g + 1)]


def unpack_kernel(packed, network_out, token_grad):
    places = [ORDER.index(g) for g in range(MEMBERS)]
    columns = jnp.concatenate([packed[i] for i in places], 0).T
    network_out[...] = columns[:UNITS]
    token_grad[...] = columns[UNITS:]


def core_sum_kernel(keep, came, pieces):
    pieces[...] = (keep[...] + came[...].astype(f32)).astype(bf16)


def piece_sum_kernel(pieces, total):
    value = pieces[0].astype(f32)
    for k in range(1, pieces.shape[0]):
        value = value + pieces[k].astype(f32)
    total[...] = value.astype(bf16)


def pair_sum_kernel(own, came, total):
    value = (own[...].astype(f32) + came[...].astype(f32)).astype(bf16)
    total[...] = jnp.broadcast_to(value, total.shape)


def finish_kernel(core, gate, mine, theirs, spread, merge, bias, gate_out, *, grad_scale):
    def write(first, second):
        for p in range(16):
            rows = slice(24 * p, 24 * (p + 1))
            for c in range(6):
                spread[rows, 128 * c : 128 * (c + 1)] = (
                    first[p, 24 * c : 24 * (c + 1), :].astype(f32) * grad_scale
                )
            rows = slice(48 * p, 48 * (p + 1))
            for c in range(3):
                merge[rows, 128 * c : 128 * (c + 1)] = (
                    second[p, 48 * c : 48 * (c + 1), :].astype(f32) * grad_scale
                )
        aux = first[0, PIECE:, :].astype(f32) * grad_scale
        gate_open = jax.nn.sigmoid(gate[...].reshape(1, SWITCH))
        slope = gate_open * (1.0 - gate_open)
        for k in range(3):
            at = slice(128 * k, 128 * (k + 1))
            bias[at] = aux[k, :]
            gate_out[at] = aux[3 + k, :] * slope[0, at]

    @pl.when(core[0] == 0)
    def _():
        write(mine, theirs)

    @pl.when(core[0] != 0)
    def _():
        write(theirs, mine)


def shaped(shape, dtype):
    return jax.ShapeDtypeStruct(shape, dtype)


def near(shape, dtype):
    return pltpu.VMEM(shape, dtype)


VMEM = pl.BlockSpec(memory_space=pltpu.VMEM)
SMEM = pl.BlockSpec(memory_space=pltpu.SMEM)


def call(kernel, outs, ins, scalars=0, scratch=(), far=False):
    arrays = ins[scalars:]
    space = pltpu.HBM if far else pltpu.VMEM
    arrays = [pltpu.with_memory_space_constraint(a, space) for a in arrays]
    return pl.pallas_call(
        kernel,
        out_shape=outs,
        in_specs=[SMEM] * scalars + [VMEM] * len(arrays),
        out_specs=tuple(VMEM for _ in outs) if isinstance(outs, tuple) else VMEM,
        scratch_shapes=list(scratch),
        compiler_params=pltpu.CompilerParams(vmem_limit_bytes=40 * 2**20),
    )(*ins[:scalars], *arrays)


def bit_groups(count, bits):
    mask = sum(1 << b for b in bits)
    groups = []
    for base in range(count):
        if base & mask:
            continue
        group = [base]
        for b in sorted(bits):
            group = group + [g | (1 << b) for g in group]
        groups.append(group)
    return groups


def exchange(value, mask):
    return lax.ppermute(value, "seq", [(i, i ^ mask) for i in range(lax.axis_size("seq"))])


def step(tokens, out_grad, spread_weight, merge_weight, switch_bias, gate_logit):
    count = lax.axis_size("seq")
    grad_scale = 1.0 / math.sqrt(count * tokens.shape[0])
    position = lax.axis_index("seq")
    core = (position % 2).astype(jnp.int32).reshape(1)
    members = [[group[g] for g in ORDER] for group in bit_groups(count, (4, 5, 6, 7))]
    planes = [
        [group[15 - (4 * i % 16 + i // 4)] for i in range(16)]
        for group in bit_groups(count, (1, 2, 6, 7))
    ]

    def swap_rows(packed):
        return lax.all_to_all(packed, "seq", 0, 0, axis_index_groups=members)

    def swap_slots(slots):
        return lax.all_to_all(slots, "seq", 0, 0, axis_index_groups=planes)

    rows = tokens.shape[0]
    packed = call(
        pack_kernel,
        near((MEMBERS, ROWS, SWITCH), bf16),
        (tokens.T, out_grad.T),
        far=True,
    )
    packed = swap_rows(packed)
    total = SECTIONS * PAIRS
    piece = (PIECE + AUX, 128)
    half = (16, *piece)
    packed_out, send, keep = call(
        switch_kernel,
        (near((MEMBERS, ROWS, SWITCH), bf16), near(half, bf16), near(half, f32)),
        (core, packed, spread_weight, merge_weight, switch_bias, gate_logit),
        1,
        [
            pltpu.VMEM((MEMBERS, ROWS, UNITS), bf16),
            pltpu.VMEM((MEMBERS, ROWS, UNITS), bf16),
            pltpu.VMEM((total, SWITCH), bf16),
            pltpu.VMEM((PAIRS, HIDDEN), f32),
            pltpu.VMEM((total, HIDDEN), f32),
            pltpu.VMEM((total, HIDDEN), f32),
            pltpu.VMEM((total, HIDDEN), bf16),
            pltpu.VMEM((total, 128), f32),
            pltpu.VMEM((total, SWITCH), bf16),
            pltpu.VMEM((PAIRS, HIDDEN), bf16),
            pltpu.VMEM((SWITCH, HIDDEN), f32),
            pltpu.VMEM((HIDDEN, SWITCH), f32),
        ],
    )
    came = exchange(send, 1)
    pieces = call(core_sum_kernel, near(half, bf16), (keep, came))
    pieces = swap_slots(pieces)
    summed = call(piece_sum_kernel, near(piece, bf16), (pieces,))
    came = exchange(summed, 8)
    packed_out = swap_rows(packed_out)
    summed = call(pair_sum_kernel, near(piece, bf16), (summed, came))
    came = exchange(summed, 16)
    summed = call(pair_sum_kernel, near(piece, bf16), (summed, came))
    came = exchange(summed, 32)
    pieces = call(pair_sum_kernel, near(half, bf16), (summed, came))
    mine = swap_slots(pieces)
    theirs = exchange(mine, 1)
    network_out, token_grad = call(
        unpack_kernel, (shaped((UNITS, rows), bf16),) * 2, (packed_out,)
    )
    spread_grad, merge_grad, bias_grad, gate_grad = call(
        lambda *refs: finish_kernel(*refs, grad_scale=grad_scale),
        (
            shaped((SWITCH, HIDDEN), f32),
            shaped((HIDDEN, SWITCH), f32),
            shaped((SWITCH,), f32),
            shaped((SWITCH,), f32),
        ),
        (core, gate_logit, mine, theirs),
        1,
    )
    return (network_out.T, token_grad.T, spread_grad, merge_grad, bias_grad, gate_grad)


def solution(mesh):
    placed = (P("seq", None), P("seq", None), P(), P(), P(), P())
    return jax.shard_map(
        step,
        mesh=mesh,
        in_specs=placed,
        out_specs=(P("seq", None), P("seq", None), P(), P(), P(), P()),
        check_vma=False,
    )
```

```python
import math

import jax
import jax.numpy as jnp
from jax import lax
from jax.experimental import pallas as pl
from jax.experimental.pallas import tpu as pltpu
from jax.sharding import PartitionSpec as P


SECTIONS = 4
MEMBERS = 16
ROWS = 32
UNITS = 192
SWITCH = 384
HIDDEN = 768
PAIRS = 256
PIECE = 144
AUX = 8
BLOCK = 32
STEPS = 2
ORDER = list(reversed(range(MEMBERS)))

sqrt_half = 0.7071067811865476
inv_sqrt_two_pi = 0.3989422804014327
f32 = jnp.float32
bf16 = jnp.bfloat16


def dot(a, b, ca, cb):
    return lax.dot_general(a, b, (((ca,), (cb,)), ((), ())), preferred_element_type=f32)


def sides(section):
    bit = MEMBERS >> (section + 1)
    lower = [g for g in range(MEMBERS) if not g & bit]
    return lower, [g + bit for g in lower]


def load_rows(ref, members):
    return jnp.concatenate([ref[g] for g in members], 0)


def store_rows(ref, members, value):
    for k, g in enumerate(members):
        ref[g] = value[ROWS * k : ROWS * (k + 1)]


def add_to(ref, section, term):
    if section == SECTIONS - 1:
        ref[...] = term
    else:
        ref[...] += term


def switch_kernel(
    core,
    packed,
    spread,
    merge,
    bias,
    gate,
    packed_out,
    send,
    keep,
    state,
    grad,
    paired,
    pre,
    normed,
    slope,
    hidden,
    scale,
    dbranch,
    dpre,
    spread_sum,
    merge_sum,
):
    gate_open = jax.nn.sigmoid(gate[...].reshape(1, SWITCH))
    bias_all = 0.25 * bias[...].reshape(1, SWITCH)
    for i, g in enumerate(ORDER):
        state[g] = packed[i, :, :UNITS]
        grad[g] = packed[i, :, UNITS:]
    for section in range(SECTIONS):
        lower, upper = sides(section)
        base = PAIRS * section
        rows = slice(base, base + PAIRS)
        paired[rows, :UNITS] = load_rows(state, lower)
        paired[rows, UNITS:] = load_rows(state, upper)
        here = paired[rows, :]
        pre[...] = dot(here, spread[...], 1, 0)
        for start in range(0, PAIRS, BLOCK):
            at = slice(start, start + BLOCK)
            to = slice(base + start, base + start + BLOCK)
            value = pre[at, :]
            centered = value - jnp.mean(value, -1, keepdims=True)
            inv = lax.rsqrt(jnp.mean(centered * centered, -1, keepdims=True) + 1e-05)
            norm = centered * inv
            cdf = 0.5 * (1.0 + lax.erf(norm * sqrt_half))
            normed[to, :] = norm
            slope[to, :] = cdf + norm * jnp.exp(-0.5 * norm * norm) * inv_sqrt_two_pi
            hidden[to, :] = (norm * cdf).astype(bf16)
            scale[to, :] = jnp.broadcast_to(inv, (BLOCK, 128))
        branch = dot(hidden[rows, :], merge[...], 1, 0)
        out = (gate_open * here.astype(f32) + (0.25 * branch + bias_all)).astype(bf16)
        store_rows(state, lower, out[:, :UNITS])
        store_rows(state, upper, out[:, UNITS:])
    for i, g in enumerate(ORDER):
        packed_out[i, :, :UNITS] = state[g]

    bias_sum = jnp.zeros((1, SWITCH), f32)
    gate_sum = jnp.zeros((1, SWITCH), f32)
    for section in reversed(range(SECTIONS)):
        lower, upper = sides(section)
        base = PAIRS * section
        rows = slice(base, base + PAIRS)
        dbranch[rows, :UNITS] = load_rows(grad, lower)
        dbranch[rows, UNITS:] = load_rows(grad, upper)
        wide = dbranch[rows, :].astype(f32)
        bias_sum += jnp.sum(wide, 0, keepdims=True)
        gate_sum += jnp.sum(wide * paired[rows, :].astype(f32), 0, keepdims=True)
        quarter = (0.25 * wide).astype(bf16)
        dbranch[rows, :] = quarter
        pre[...] = dot(quarter, merge[...], 1, 1)
        add_to(merge_sum, section, dot(hidden[rows, :], quarter, 0, 0))
        for start in range(0, PAIRS, BLOCK):
            at = slice(start, start + BLOCK)
            to = slice(base + start, base + start + BLOCK)
            norm = normed[to, :]
            dn = pre[at, :] * slope[to, :]
            mean = jnp.mean(dn, -1, keepdims=True)
            along = jnp.mean(dn * norm, -1, keepdims=True)
            inv = scale[to, :][:, :1]
            dpre[at, :] = (inv * (dn - mean - norm * along)).astype(bf16)
        back = dpre[...]
        total = (gate_open * wide + dot(back, spread[...], 1, 1)).astype(bf16)
        store_rows(grad, lower, total[:, :UNITS])
        store_rows(grad, upper, total[:, UNITS:])
        add_to(spread_sum, section, dot(paired[rows, :], back, 0, 0))
    for i, g in enumerate(ORDER):
        packed_out[i, :, UNITS:] = grad[g]

    bias_row = 0.25 * bias_sum
    gate_row = gate_sum
    aux = jnp.concatenate(
        [row[:, 128 * k : 128 * (k + 1)] for row in (bias_row, gate_row) for k in range(3)]
        + [jnp.zeros((2, 128), f32)],
        0,
    )

    def put_spread(ref):
        for p in range(16):
            for c in range(6):
                ref[p, 24 * c : 24 * (c + 1), :] = spread_sum[
                    24 * p : 24 * (p + 1), 128 * c : 128 * (c + 1)
                ].astype(ref.dtype)
        ref[0, PIECE:, :] = aux.astype(ref.dtype)
        ref[1:, PIECE:, :] = jnp.zeros((15, AUX, 128), ref.dtype)

    def put_merge(ref):
        for p in range(16):
            for c in range(3):
                ref[p, 48 * c : 48 * (c + 1), :] = merge_sum[
                    48 * p : 48 * (p + 1), 128 * c : 128 * (c + 1)
                ].astype(ref.dtype)
        ref[:, PIECE:, :] = jnp.zeros((16, AUX, 128), ref.dtype)

    @pl.when(core[0] == 0)
    def _():
        put_spread(keep)
        put_merge(send)

    @pl.when(core[0] != 0)
    def _():
        put_merge(keep)
        put_spread(send)


def pack_kernel(tokens, out_grad, packed):
    rows = jnp.concatenate([tokens[...], out_grad[...]], 0).T
    for k in range(MEMBERS // STEPS):
        packed[MEMBERS // STEPS - 1 - k] = rows[ROWS * k : ROWS * (k + 1)]


def unpack_kernel(packed, network_out, token_grad):
    places = [ORDER.index(g) for g in range(MEMBERS)]
    columns = jnp.concatenate([packed[i] for i in places], 0).T
    network_out[...] = columns[:UNITS]
    token_grad[...] = columns[UNITS:]


def core_sum_kernel(keep, came, pieces):
    pieces[...] = (keep[...] + came[...].astype(f32)).astype(bf16)


def piece_sum_kernel(pieces, total):
    value = pieces[0].astype(f32)
    for k in range(1, pieces.shape[0]):
        value = value + pieces[k].astype(f32)
    total[...] = value.astype(bf16)


def pair_sum_kernel(own, came, total):
    value = (own[...].astype(f32) + came[...].astype(f32)).astype(bf16)
    total[...] = jnp.broadcast_to(value, total.shape)


def finish_kernel(core, gate, mine, theirs, spread, merge, bias, gate_out, *, grad_scale):
    step = pl.program_id(0)
    each = 16 // STEPS

    def write(first, second):
        for k in range(each):
            rows = slice(24 * k, 24 * (k + 1))
            for c in range(6):
                spread[rows, 128 * c : 128 * (c + 1)] = (
                    first[each * step + k, 24 * c : 24 * (c + 1), :].astype(f32) * grad_scale
                )
            rows = slice(48 * k, 48 * (k + 1))
            for c in range(3):
                merge[rows, 128 * c : 128 * (c + 1)] = (
                    second[each * step + k, 48 * c : 48 * (c + 1), :].astype(f32) * grad_scale
                )

        @pl.when(step == 0)
        def _():
            aux = first[0, PIECE:, :].astype(f32) * grad_scale
            gate_open = jax.nn.sigmoid(gate[...].reshape(1, SWITCH))
            slope = gate_open * (1.0 - gate_open)
            for k in range(3):
                at = slice(128 * k, 128 * (k + 1))
                bias[at] = aux[k, :]
                gate_out[at] = aux[3 + k, :] * slope[0, at]

    @pl.when(core[0] == 0)
    def _():
        write(mine, theirs)

    @pl.when(core[0] != 0)
    def _():
        write(theirs, mine)


def shaped(shape, dtype):
    return jax.ShapeDtypeStruct(shape, dtype)


def near(shape, dtype):
    return pltpu.VMEM(shape, dtype)


VMEM = pl.BlockSpec(memory_space=pltpu.VMEM)
SMEM = pl.BlockSpec(memory_space=pltpu.SMEM)


def call(kernel, outs, ins, scalars=0, scratch=(), far=False, grid=(), blocks=None):
    arrays = ins[scalars:]
    space = pltpu.HBM if far else pltpu.VMEM
    arrays = [pltpu.with_memory_space_constraint(a, space) for a in arrays]
    return pl.pallas_call(
        kernel,
        out_shape=outs,
        grid=grid,
        in_specs=blocks[0] if blocks else [SMEM] * scalars + [VMEM] * len(arrays),
        out_specs=blocks[1]
        if blocks
        else tuple(VMEM for _ in outs)
        if isinstance(outs, tuple)
        else VMEM,
        scratch_shapes=list(scratch),
        compiler_params=pltpu.CompilerParams(vmem_limit_bytes=40 * 2**20),
    )(*ins[:scalars], *arrays)


def bit_groups(count, bits):
    mask = sum(1 << b for b in bits)
    groups = []
    for base in range(count):
        if base & mask:
            continue
        group = [base]
        for b in sorted(bits):
            group = group + [g | (1 << b) for g in group]
        groups.append(group)
    return groups


def exchange(value, mask):
    return lax.ppermute(value, "seq", [(i, i ^ mask) for i in range(lax.axis_size("seq"))])


def step(tokens, out_grad, spread_weight, merge_weight, switch_bias, gate_logit):
    count = lax.axis_size("seq")
    grad_scale = 1.0 / math.sqrt(count * tokens.shape[0])
    position = lax.axis_index("seq")
    core = (position % 2).astype(jnp.int32).reshape(1)
    members = [[group[g] for g in ORDER] for group in bit_groups(count, (4, 5, 6, 7))]
    planes = [
        [group[15 - (4 * i % 16 + i // 4)] for i in range(16)]
        for group in bit_groups(count, (1, 2, 6, 7))
    ]

    def swap_rows(packed):
        return lax.all_to_all(packed, "seq", 0, 0, axis_index_groups=members)

    def swap_slots(slots):
        return lax.all_to_all(slots, "seq", 0, 0, axis_index_groups=planes)

    rows = tokens.shape[0]
    packed = call(
        pack_kernel,
        near((MEMBERS, ROWS, SWITCH), bf16),
        (tokens.T, out_grad.T),
        far=True,
        grid=(STEPS,),
        blocks=(
            [pl.BlockSpec((UNITS, rows // STEPS), lambda i: (0, i))] * 2,
            pl.BlockSpec((MEMBERS // STEPS, ROWS, SWITCH), lambda i: (STEPS - 1 - i, 0, 0)),
        ),
    )
    packed = swap_rows(packed)
    total = SECTIONS * PAIRS
    piece = (PIECE + AUX, 128)
    half = (16, *piece)
    packed_out, send, keep = call(
        switch_kernel,
        (near((MEMBERS, ROWS, SWITCH), bf16), near(half, bf16), near(half, f32)),
        (core, packed, spread_weight, merge_weight, switch_bias, gate_logit),
        1,
        [
            pltpu.VMEM((MEMBERS, ROWS, UNITS), bf16),
            pltpu.VMEM((MEMBERS, ROWS, UNITS), bf16),
            pltpu.VMEM((total, SWITCH), bf16),
            pltpu.VMEM((PAIRS, HIDDEN), f32),
            pltpu.VMEM((total, HIDDEN), f32),
            pltpu.VMEM((total, HIDDEN), f32),
            pltpu.VMEM((total, HIDDEN), bf16),
            pltpu.VMEM((total, 128), f32),
            pltpu.VMEM((total, SWITCH), bf16),
            pltpu.VMEM((PAIRS, HIDDEN), bf16),
            pltpu.VMEM((SWITCH, HIDDEN), f32),
            pltpu.VMEM((HIDDEN, SWITCH), f32),
        ],
    )
    came = exchange(send, 1)
    pieces = call(core_sum_kernel, near(half, bf16), (keep, came))
    pieces = swap_slots(pieces)
    summed = call(piece_sum_kernel, near(piece, bf16), (pieces,))
    came = exchange(summed, 8)
    packed_out = swap_rows(packed_out)
    summed = call(pair_sum_kernel, near(piece, bf16), (summed, came))
    came = exchange(summed, 16)
    summed = call(pair_sum_kernel, near(piece, bf16), (summed, came))
    came = exchange(summed, 32)
    pieces = call(pair_sum_kernel, near(half, bf16), (summed, came))
    mine = swap_slots(pieces)
    theirs = exchange(mine, 1)
    network_out, token_grad = call(unpack_kernel, (shaped((UNITS, rows), bf16),) * 2, (packed_out,))
    spread_grad, merge_grad, bias_grad, gate_grad = call(
        lambda *refs: finish_kernel(*refs, grad_scale=grad_scale),
        (
            shaped((SWITCH, HIDDEN), f32),
            shaped((HIDDEN, SWITCH), f32),
            shaped((SWITCH,), f32),
            shaped((SWITCH,), f32),
        ),
        (core, gate_logit, mine, theirs),
        1,
        grid=(STEPS,),
        blocks=(
            [SMEM, VMEM, VMEM, VMEM],
            (
                pl.BlockSpec((SWITCH // STEPS, HIDDEN), lambda i: (i, 0)),
                pl.BlockSpec((HIDDEN // STEPS, SWITCH), lambda i: (i, 0)),
                pl.BlockSpec((SWITCH,), lambda i: (0,)),
                pl.BlockSpec((SWITCH,), lambda i: (0,)),
            ),
        ),
    )
    return (network_out.T, token_grad.T, spread_grad, merge_grad, bias_grad, gate_grad)


def solution(mesh):
    placed = (P("seq", None), P("seq", None), P(), P(), P(), P())
    return jax.shard_map(
        step,
        mesh=mesh,
        in_specs=placed,
        out_specs=(P("seq", None), P("seq", None), P(), P(), P(), P()),
        check_vma=False,
    )
```
